32 devices in a mesh: pipe: 2 (over x), ctx: 4 (over y, core), tp: 4 (over z).
Axes of the slice: x: 2, y: 2, z: 4, core: 2. Of those that a mesh axis runs over, the one named last changes fastest.
Arguments:
- queries: bfloat16 [2, 512, 16384], P('pipe', 'ctx', 'tp'), may hold values from -5 to 5
- key_vectors: bfloat16 [2, 512, 1024], P('pipe', 'ctx', 'tp'), may hold values from -5 to 5
- saved_value_rows: bfloat16 [2, 512, 1024], P('pipe', 'ctx', 'tp'), may hold values from -5 to 5
- output_cotangent: bfloat16 [2, 512, 16384], P('pipe', 'ctx', 'tp'), may hold values from -5 to 5
- layer_input: bfloat16 [2, 512, 8192], P('pipe', 'ctx'), may hold values from -5 to 5
- documents: int32 [2, 512], P('pipe'), may hold values from 0 to 3, as said below
Outputs:
- query_gradient: bfloat16 [2, 512, 16384], P('pipe', 'ctx', 'tp')
- key_gradient: bfloat16 [2, 512, 1024], P('pipe', 'ctx', 'tp')
- value_gradient: bfloat16 [2, 512, 1024], P('pipe', 'ctx', 'tp')
- weight_gradient: float32 [2, 8192, 1024], P('pipe', 'ctx', 'tp')
The draws below stay inside these ranges and needn't reach their ends.
Inputs may be any that keep to these rules, and one draw needn't show every extreme that they name: For each section, the numbers start at 0 on the first token and never fall along the tokens; each of the 4 documents has one token or more.
All inputs are finite; a program needn't handle non-finite values.
Results may differ from the reference program's by a relative error of at most 0.0095.
Values may be sent and summed in bfloat16 or wider, within the bound.
No kernel may reach another device: no remote copies, remote signals or barrier semaphores. Data moves between devices by JAX's collectives and lax.ppermute only.
A program may use at most 64 MiB of HBM per device.

```python
import math
import jax
import jax.numpy as jnp
from jax import lax

QUERY_HEADS = 128
KEY_VALUE_HEADS = 8
HEAD_SIZE = 128
DW = 8192
DOCS = 4
RELAY_SECTIONS = 2
MICRO_TOKENS = 512


def make_documents(key):
    base_key = jax.random.fold_in(key, 7)
    section_keys = jax.random.split(base_key, RELAY_SECTIONS)

    def one_section(relay_key):
        shuffled = jax.random.permutation(relay_key, MICRO_TOKENS - 1) + 1
        cut_points = shuffled[:DOCS - 1]
        start_flags = jnp.zeros((MICRO_TOKENS,), jnp.int32).at[cut_points].set(1)
        return jnp.cumsum(start_flags).astype(jnp.int32)
    return jax.vmap(one_section)(section_keys)


def draw_documents(key, part):
    return make_documents(key)


def draw_queries(key, part):
    query_key = jax.random.fold_in(key, 41)
    picked_rows = jnp.clip(jax.random.normal(query_key, (RELAY_SECTIONS, MICRO_TOKENS, QUERY_HEADS, HEAD_SIZE), jnp.float32), -4.5, 4.5)
    return picked_rows.reshape(RELAY_SECTIONS, MICRO_TOKENS, QUERY_HEADS * HEAD_SIZE).astype(jnp.bfloat16)


def draw_key_vectors(key, part):
    random_key = jax.random.fold_in(key, 53)
    picked_rows = jnp.clip(jax.random.normal(random_key, (RELAY_SECTIONS, MICRO_TOKENS, KEY_VALUE_HEADS, HEAD_SIZE), jnp.float32), -4.5, 4.5)
    return picked_rows.reshape(RELAY_SECTIONS, MICRO_TOKENS, KEY_VALUE_HEADS * HEAD_SIZE).astype(jnp.bfloat16)


def steps_of(stream_key, dims, shards, smallest, largest):
    def one(dim, blocks):
        heights = jax.random.uniform(jax.random.fold_in(jax.random.fold_in(stream_key, 6), dim), (blocks,), jnp.float32, smallest / len(shards), largest / len(shards))
        return jnp.repeat(jnp.exp(heights), dims[dim] // blocks).reshape((-1,) + (1,) * (len(dims) - dim - 1))

    gain = one(*shards[0])
    for cut in shards[1:]:
        gain = gain * one(*cut)
    return gain


def bell_draw(key, extent, deviation, limit, cuts=(), kind=jnp.bfloat16):
    values = jax.random.normal(key, extent, jnp.float32) * deviation
    if len(cuts) > 0:
        values = steps_of(key, extent, cuts, -0.22, 0.18) * values
    return jnp.clip(values, min=-limit, max=limit).astype(kind)


def setup_inputs(seed: int = 0) -> dict:
    key_list = jax.random.split(jax.random.key(seed), 7)
    queries = draw_queries(jax.random.fold_in(key_list[6], 71), 0)
    key_vectors = draw_key_vectors(jax.random.fold_in(key_list[6], 71), 0)
    saved_value_rows = bell_draw(key_list[2], (RELAY_SECTIONS, MICRO_TOKENS, KEY_VALUE_HEADS * HEAD_SIZE), 1.0, 5.0, ((0, 2), (1, 4), (2, 4)))
    output_cotangent = bell_draw(key_list[3], (RELAY_SECTIONS, MICRO_TOKENS, QUERY_HEADS * HEAD_SIZE), 1.0, 5.0, ((0, 2), (1, 4), (2, 4)))
    layer_input = bell_draw(key_list[4], (RELAY_SECTIONS, MICRO_TOKENS, DW), 1.0, 5.0, ((0, 2), (1, 4)))
    documents = draw_documents(jax.random.fold_in(key_list[6], 71), 0)
    return {"queries": queries, "key_vectors": key_vectors, "saved_value_rows": saved_value_rows, "output_cotangent": output_cotangent, "layer_input": layer_input, "documents": documents}


def attend(query_rows, cotangent_rows, keys_one, values_one, query_position, query_documents, key_documents, scaling):
    row_count = query_rows.shape[0]
    head_width = query_rows.shape[1]
    block_rows = math.gcd(row_count, 512)
    block_count = row_count // block_rows
    key_count = keys_one.shape[0]
    key_position = jnp.arange(key_count, dtype=jnp.int32)

    def advance(totals, pieces):
        key_total, value_total = totals
        block_query, block_cotangent, block_position, block_documents = pieces
        scores = jnp.einsum("rd,kd->rk", block_query, keys_one, preferred_element_type=jnp.float32) * scaling
        allowed = (block_documents[:, None] == key_documents[None, :]) & (key_position[None, :] <= block_position[:, None])
        masked = jnp.where(allowed, scores, -1e30)
        row_max = jnp.max(masked, axis=1, keepdims=True)
        raised = jnp.where(allowed, jnp.exp(masked - row_max), 0.0)
        weights = raised / jnp.sum(raised, axis=1, keepdims=True)
        weights_low = weights.astype(jnp.bfloat16)
        attended = jnp.dot(weights_low, values_one, preferred_element_type=jnp.float32)
        row_delta = jnp.sum(block_cotangent.astype(jnp.float32) * attended, axis=1, keepdims=True)
        weights_back = jnp.einsum("rd,kd->rk", block_cotangent, values_one, preferred_element_type=jnp.float32)
        scores_back = weights * (weights_back - row_delta)
        scores_low = scores_back.astype(jnp.bfloat16)
        query_part = jnp.dot(scores_low, keys_one, preferred_element_type=jnp.float32) * scaling
        key_total = key_total + jnp.einsum("rk,rd->kd", scores_low, block_query, preferred_element_type=jnp.float32) * scaling
        value_total = value_total + jnp.einsum("rk,rd->kd", weights_low, block_cotangent, preferred_element_type=jnp.float32)
        return (key_total, value_total), query_part

    zero_init = jnp.zeros((key_count, head_width), jnp.float32)
    stacked = (query_rows.reshape(block_count, block_rows, head_width),
               cotangent_rows.reshape(block_count, block_rows, head_width),
               query_position.reshape(block_count, block_rows),
               query_documents.reshape(block_count, block_rows))
    (key_total, value_total), query_parts = lax.scan(advance, (zero_init, zero_init), stacked)
    return query_parts.reshape(row_count, head_width), key_total, value_total


def reference(queries, key_vectors, saved_value_rows, output_cotangent, layer_input, documents):
    query_group = QUERY_HEADS // KEY_VALUE_HEADS
    scaling = HEAD_SIZE ** -0.5

    def per_section(pieces):
        relay_query, relay_key, relay_value, relay_cotangent, section_documents = pieces
        headwise_queries = relay_query.reshape(MICRO_TOKENS, KEY_VALUE_HEADS, query_group, HEAD_SIZE).transpose(1, 2, 0, 3).reshape(KEY_VALUE_HEADS, query_group * MICRO_TOKENS, HEAD_SIZE)
        headwise_cotangent = relay_cotangent.reshape(MICRO_TOKENS, KEY_VALUE_HEADS, query_group, HEAD_SIZE).transpose(1, 2, 0, 3).reshape(KEY_VALUE_HEADS, query_group * MICRO_TOKENS, HEAD_SIZE)
        headwise_keys = relay_key.reshape(MICRO_TOKENS, KEY_VALUE_HEADS, HEAD_SIZE).transpose(1, 0, 2)
        headwise_values = relay_value.reshape(MICRO_TOKENS, KEY_VALUE_HEADS, HEAD_SIZE).transpose(1, 0, 2)
        positions = jnp.tile(jnp.arange(MICRO_TOKENS, dtype=jnp.int32), query_group)
        row_documents = jnp.tile(section_documents, query_group)

        def per_head(head_pieces):
            head_query, head_cotangent, head_key, head_value = head_pieces
            return attend(head_query, head_cotangent, head_key, head_value, positions, row_documents, section_documents, scaling)

        query_gradient_sum, key_gradient_sum, value_gradient_sum = lax.map(per_head, (headwise_queries, headwise_cotangent, headwise_keys, headwise_values))
        query_result = query_gradient_sum.reshape(KEY_VALUE_HEADS, query_group, MICRO_TOKENS, HEAD_SIZE).transpose(2, 0, 1, 3).reshape(MICRO_TOKENS, QUERY_HEADS * HEAD_SIZE)
        key_result = key_gradient_sum.transpose(1, 0, 2).reshape(MICRO_TOKENS, KEY_VALUE_HEADS * HEAD_SIZE)
        value_result = value_gradient_sum.transpose(1, 0, 2).reshape(MICRO_TOKENS, KEY_VALUE_HEADS * HEAD_SIZE)
        return query_result.astype(jnp.bfloat16), key_result.astype(jnp.bfloat16), value_result.astype(jnp.bfloat16)

    query_gradient, key_gradient, value_gradient = lax.map(per_section, (queries, key_vectors, saved_value_rows, output_cotangent, documents))
    incoming = jnp.roll(layer_input, 1, axis=0)

    def weight_section(pieces):
        input_section, key_section = pieces
        return lax.dot_general(input_section, key_section, (((0,), (0,)), ((), ())), preferred_element_type=jnp.float32)

    weight_gradient = lax.map(weight_section, (incoming, key_gradient))
    return query_gradient, key_gradient, value_gradient, weight_gradient
```

```python
import functools
import math

import jax
import jax.numpy as jnp
from jax import lax
from jax.experimental import pallas as pl
from jax.experimental.pallas import tpu as pltpu
from jax.sharding import PartitionSpec as P

QUERY_HEADS = 128
KEY_VALUE_HEADS = 8
HEAD_SIZE = 128
DOCS = 4

ROWS = (((1,), (1,)), ((), ()))
PLAIN = (((1,), (0,)), ((), ()))
COLUMNS = (((0,), (0,)), ((), ()))


def product(a, b, dims):
    return lax.dot_general(a, b, dims, preferred_element_type=jnp.float32)


def swapped(block, axis, mask):
    count = lax.axis_size(axis)
    return lax.ppermute(block, axis, [(i, i ^ mask) for i in range(count)])


def handed_on(block, section_axis, token_axis, mask):
    sections, count = lax.axis_size(section_axis), lax.axis_size(token_axis)
    route = [
        (s * count + i, ((s + 1) % sections) * count + (i ^ mask))
        for s in range(sections)
        for i in range(count)
    ]
    return lax.ppermute(block, (section_axis, token_axis), route)


def spans(count):
    return [s for s in range(1, count + 1) if s <= 4 or s & (s - 1) == 0 or s == count]


def attention_kernel(
    count,
    group,
    scaling,
    facts,
    query_ref,
    cotangent_ref,
    *rest,
):
    pair_refs = rest[:count]
    query_out, key_keep, key_send, value_keep, value_send = rest[count : count + 5]
    keys, values, keys_turned, bias, key_total, value_total = rest[count + 5 :]
    tokens = query_ref.shape[0]
    step = pl.program_id(1)
    place = facts[0]
    factor = scaling * math.log2(math.e)

    first_block = facts[1]
    needed = place - first_block + 1
    branches = spans(count)

    @pl.when(step == 0)
    def _():
        for slot in range(count):
            row = pl.multiple_of((place ^ slot) * tokens, tokens)
            keys[pl.ds(row, tokens), :] = pair_refs[slot][:tokens, :]
            values[pl.ds(row, tokens), :] = pair_refs[slot][tokens:, :]
        key_total[...] = jnp.zeros_like(key_total)
        value_total[...] = jnp.zeros_like(value_total)

    def work(span):
        start_block = jnp.minimum(first_block, count - span)
        start = pl.multiple_of(start_block * tokens, tokens)
        length = span * tokens
        window = pl.ds(start, length)

        @pl.when(step == 0)
        def _():
            key_position = start + lax.broadcasted_iota(jnp.int32, (length, tokens), 0)
            query_position = place * tokens + lax.broadcasted_iota(jnp.int32, (length, tokens), 1)
            opening = jnp.zeros((length, tokens), jnp.int32)
            for d in range(DOCS - 1):
                bound = facts[2 + d]
                opening = jnp.where(query_position >= bound, jnp.maximum(opening, bound), opening)
            allowed = (key_position <= query_position) & (key_position >= opening)
            bias[:length, :] = jnp.where(allowed, 0.0, -1e30)
            keys_turned[:, :length] = keys[window, :].astype(jnp.float32).T.astype(jnp.bfloat16)

        key_rows = keys[window, :]
        value_rows = values[window, :]
        rows = [slice(g * HEAD_SIZE, (g + 1) * HEAD_SIZE) for g in range(group)]
        query_rows = jnp.concatenate([query_ref[:, r] for r in rows], axis=0)
        cotangent_rows = jnp.concatenate([cotangent_ref[:, r] for r in rows], axis=0)
        scores_all = product(key_rows, query_rows, ROWS)
        back_all = product(value_rows, cotangent_rows, ROWS)
        low_list = []
        back_list = []
        for g in range(group):
            lanes = slice(g * tokens, (g + 1) * tokens)
            scores = scores_all[:, lanes] + bias[:length, :]
            top = jnp.max(scores, axis=0, keepdims=True)
            raised = jnp.exp2((scores - top) * factor)
            weights = raised * (1.0 / jnp.sum(raised, axis=0, keepdims=True))
            back = back_all[:, lanes]
            delta = jnp.sum(weights * back, axis=0, keepdims=True)
            low_list.append(weights.astype(jnp.bfloat16))
            back_list.append((weights * (back - delta)).astype(jnp.bfloat16))
        weights_low = jnp.concatenate(low_list, axis=1)
        scores_low = jnp.concatenate(back_list, axis=1)
        value_total[window, :] += product(weights_low, cotangent_rows, PLAIN)
        key_total[window, :] += product(scores_low, query_rows, PLAIN)
        turned = product(keys_turned[:, :length], scores_low, PLAIN) * scaling
        for g in range(group):
            query_out[:, rows[g]] = turned[:, g * tokens : (g + 1) * tokens].T.astype(
                query_out.dtype
            )

    for i, span in enumerate(branches):
        below = branches[i - 1] if i else 0
        pl.when((needed > below) & (needed <= span))(functools.partial(work, span))

    @pl.when(step == pl.num_programs(1) - 1)
    def _():
        for slot in range(count):
            row = pl.multiple_of((place ^ slot) * tokens, tokens)
            half = pl.ds((slot // 2) * tokens, tokens)
            key_out, value_out = (key_send, value_send) if slot % 2 else (key_keep, value_keep)
            key_out[half, :] = (key_total[pl.ds(row, tokens), :] * scaling).astype(key_out.dtype)
            value_out[half, :] = value_total[pl.ds(row, tokens), :].astype(value_out.dtype)


def attention(facts, queries, cotangent, pairs, scaling, group):
    tokens = queries.shape[0]
    count = len(pairs)
    local_kv = pairs[0].shape[1] // HEAD_SIZE
    per_kv = queries.shape[1] // HEAD_SIZE // local_kv
    groups = per_kv // group
    wide = group * HEAD_SIZE
    half = count // 2 * tokens
    by_head = pl.BlockSpec((tokens, wide), lambda e, g, f: (0, e * groups + g))
    by_kv = pl.BlockSpec((2 * tokens, HEAD_SIZE), lambda e, g, f: (0, e))
    terms = pl.BlockSpec((half, HEAD_SIZE), lambda e, g, f: (0, e))
    term_shape = (half, local_kv * HEAD_SIZE)
    heads = local_kv * per_kv
    work = heads * tokens * tokens * count * HEAD_SIZE
    return pl.pallas_call(
        functools.partial(attention_kernel, count, group, scaling),
        grid_spec=pltpu.PrefetchScalarGridSpec(
            num_scalar_prefetch=1,
            grid=(local_kv, groups),
            in_specs=[by_head, by_head] + [by_kv] * count,
            out_specs=[by_head, terms, terms, terms, terms],
            scratch_shapes=[
                pltpu.VMEM((count * tokens, HEAD_SIZE), jnp.bfloat16),
                pltpu.VMEM((count * tokens, HEAD_SIZE), jnp.bfloat16),
                pltpu.VMEM((HEAD_SIZE, count * tokens), jnp.bfloat16),
                pltpu.VMEM((count * tokens, tokens), jnp.float32),
                pltpu.VMEM((count * tokens, HEAD_SIZE), jnp.float32),
                pltpu.VMEM((count * tokens, HEAD_SIZE), jnp.float32),
            ],
        ),
        out_shape=[
            jax.ShapeDtypeStruct(queries.shape, queries.dtype),
            jax.ShapeDtypeStruct(term_shape, jnp.float32),
            jax.ShapeDtypeStruct(term_shape, jnp.bfloat16),
            jax.ShapeDtypeStruct(term_shape, jnp.float32),
            jax.ShapeDtypeStruct(term_shape, jnp.bfloat16),
        ],
        compiler_params=pltpu.CompilerParams(dimension_semantics=("arbitrary", "arbitrary")),
        cost_estimate=pl.CostEstimate(
            flops=10 * work,
            transcendentals=work // HEAD_SIZE,
            bytes_accessed=6 * queries.size + 16 * half * local_kv * HEAD_SIZE,
        ),
        name="attention_back",
    )(facts, queries, cotangent, *pairs)


def weight_kernel(count, *refs):
    incoming_refs, key_refs, out = refs[:count], refs[count:-1], refs[-1]
    per_ref = count // len(key_refs)
    tokens = incoming_refs[0].shape[0]
    total = None
    for slot in range(count):
        block = slot % per_ref
        key_rows = key_refs[slot // per_ref][block * tokens : (block + 1) * tokens, :]
        term = product(incoming_refs[slot][...], key_rows, COLUMNS)
        total = term if total is None else total + term
    out[...] = total


def weight_product(incoming, key_parts, tile):
    tokens, features = incoming[0].shape
    width = key_parts[0].shape[1]
    return pl.pallas_call(
        functools.partial(weight_kernel, len(incoming)),
        grid=(features // tile,),
        in_specs=[pl.BlockSpec((tokens, tile), lambda i: (0, i)) for _ in incoming]
        + [pl.BlockSpec(k.shape, lambda i: (0, 0)) for k in key_parts],
        out_specs=pl.BlockSpec((tile, width), lambda i: (i, 0)),
        out_shape=jax.ShapeDtypeStruct((features, width), jnp.float32),
        compiler_params=pltpu.CompilerParams(dimension_semantics=("arbitrary",)),
        cost_estimate=pl.CostEstimate(
            flops=2 * len(incoming) * tokens * features * width,
            transcendentals=0,
            bytes_accessed=2 * len(incoming) * tokens * features + 4 * features * width,
        ),
        name="weight_product",
    )(*incoming, *key_parts)


def shards(queries, key_vectors, saved_value_rows, output_cotangent, layer_input, documents):
    count = lax.axis_size("ctx")
    place = lax.axis_index("ctx")
    tokens = queries.shape[1]
    scaling = HEAD_SIZE ** (-0.5)
    features = layer_input.shape[2] // count

    pairs = {0: jnp.concatenate([key_vectors[0], saved_value_rows[0]], axis=0)}
    bits = [1 << b for b in range(count.bit_length() - 1)]
    for bit in reversed(bits):
        for slot in sorted(pairs):
            pairs[slot | bit] = swapped(pairs[slot], "ctx", bit)

    incoming = {}
    for slot in reversed(range(count)):
        block = lax.dynamic_slice_in_dim(layer_input[0], (place ^ slot) * features, features, axis=1)
        incoming[slot] = handed_on(block, "pipe", "ctx", slot)

    numbers = documents[0]
    bounds = jnp.sum(numbers[None, :] < jnp.arange(1, DOCS)[:, None], axis=1, dtype=jnp.int32)
    first = jnp.max(jnp.where(bounds <= place * tokens, bounds, 0)) // tokens
    facts = jnp.concatenate([jnp.stack([place, first]).astype(jnp.int32), bounds])

    query_gradient, key_keep, key_send, value_keep, value_send = attention(
        facts, queries[0], output_cotangent[0], [pairs[s] for s in range(count)], scaling, 4
    )

    stride = key_keep.shape[1]
    for bit in bits:
        blocks = key_keep.shape[0] // tokens
        if bit > 1:
            split_key = key_keep.reshape(blocks // 2, 2, tokens, stride)
            split_value = value_keep.reshape(blocks // 2, 2, tokens, stride)
            key_keep, key_send = (split_key[:, b].reshape(-1, stride) for b in (0, 1))
            value_keep, value_send = (split_value[:, b].reshape(-1, stride) for b in (0, 1))
        if bit == bits[-1]:
            break
        got_key = swapped(key_send.astype(jnp.bfloat16), "ctx", bit)
        got_value = swapped(value_send.astype(jnp.bfloat16), "ctx", bit)
        key_keep = key_keep + got_key.astype(jnp.float32)
        value_keep = value_keep + got_value.astype(jnp.float32)
    top = bits[-1]
    both = jnp.concatenate([key_send, key_keep], axis=0).astype(jnp.bfloat16)
    key_both = jnp.concatenate([key_keep, key_send], axis=0) + swapped(both, "ctx", top)
    key_both = key_both.astype(jnp.bfloat16)
    value_sum = value_keep + swapped(value_send.astype(jnp.bfloat16), "ctx", top)
    key_gradient = key_both[:tokens]
    value_gradient = value_sum.astype(jnp.bfloat16)

    key_parts = {0: key_both}
    for bit in reversed(bits[:-1]):
        for slot in sorted(key_parts):
            key_parts[slot | bit] = swapped(key_parts[slot], "ctx", bit)
    order = [base | extra for base in sorted(key_parts) for extra in (0, top)]
    weight_gradient = weight_product(
        [incoming[s] for s in order],
        [key_parts[b] for b in sorted(key_parts)],
        math.gcd(features, 256),
    )
    return (query_gradient[None], key_gradient[None], value_gradient[None], weight_gradient[None])


def solution(mesh):
    split = P("pipe", "ctx", "tp")
    return jax.shard_map(
        shards,
        mesh=mesh,
        in_specs=(split, split, split, split, P("pipe", "ctx", None), P("pipe", None)),
        out_specs=(split, split, split, split),
        check_vma=False,
    )
```
